128 devices in a mesh: leaf: 128 (over z, y, x, core).
Axes of the slice: x: 4, y: 4, z: 4, core: 2. Of those that a mesh axis runs over, the one named last changes fastest.
Arguments:
- shots: float32 [131072, 2048], P('leaf'), may hold values from -6 to 6
- leaf_inverse: float32 [131072, 1024], P('leaf'), may hold values from -0.1875 to 0.1875
- leaf_basis: float32 [32768, 1024], P('leaf'), may hold values from -0.1875 to 0.1875
- leaf_back: float32 [131072, 256], P('leaf'), may hold values from -0.375 to 0.375
- level_one: float32 [32768, 1024], P('leaf'), may hold values from -0.25 to 0.25
- level_two: float32 [16384, 1024], P('leaf'), may hold values from -0.25 to 0.25
- level_three: float32 [8192, 1024], P('leaf'), may hold values from -0.25 to 0.25
- top_inverse: float32 [4096, 4096], P('leaf'), may hold values from -0.1 to 0.1, as said below
Outputs:
- solution: float32 [131072, 2048], P('leaf')
The draws below stay inside these ranges and needn't reach their ends.
Inputs may be any that keep to these rules, and one draw needn't show every extreme that they name: top_inverse is symmetric.
All inputs are finite; a program needn't handle non-finite values.
Results may differ from the reference program's by a relative error of at most 0.0001.
Values sent between devices are 32-bit elements; how exact they have to be, the bound alone decides.
No kernel may reach another device: no remote copies, remote signals or barrier semaphores. Data moves between devices by JAX's collectives and lax.ppermute only.
A program may use at most 128 MiB of HBM per device.

```python
import math
import jax
import jax.numpy as jnp
from jax import lax

LEAF_ROWS = 1024
LOW_RANK = 256
SHOT_COUNT = 2048
TOP_NODES = 16
N_LEAF = 128


def draw_top_inverse(key, part):
    order = TOP_NODES * LOW_RANK
    entries = jax.random.normal(key, (order, order), jnp.float32)
    symmetric = (entries + entries.T) * (0.5 ** 0.5 / math.sqrt(order))
    return jnp.clip(symmetric, -0.1, 0.1)


def block_scale(key, shape, cuts, smallest, largest):
    level, own = 1.0, jax.random.fold_in(key, 6)
    for axis_at, parts in cuts:
        draws = jnp.exp(jax.random.uniform(jax.random.fold_in(own, axis_at), (parts,), jnp.float32, smallest / len(cuts), largest / len(cuts)))
        level = level * jnp.repeat(draws, shape[axis_at] // parts).reshape([-1 if axis == axis_at else 1 for axis in range(len(shape))])
    return level


def gaussian(rng, extent, scale, bound, split=(), held_as=jnp.bfloat16):
    values = jax.random.normal(rng, extent, jnp.float32) * scale
    if len(split) > 0:
        values = block_scale(rng, extent, split, -0.22, 0.18) * values
    return jnp.clip(values, min=-bound, max=bound).astype(held_as)


def setup_inputs(seed: int = 0) -> dict:
    streams_of = jax.random.split(jax.random.key(seed), 9)
    shots = gaussian(streams_of[0], (N_LEAF * LEAF_ROWS, SHOT_COUNT), 1.0, 6.0, ((0, 128),), jnp.float32)
    leaf_inverse = gaussian(streams_of[1], (N_LEAF * LEAF_ROWS, LEAF_ROWS), LEAF_ROWS ** -0.5, 0.1875, ((0, 128),), jnp.float32)
    leaf_basis = gaussian(streams_of[2], (N_LEAF * LOW_RANK, LEAF_ROWS), LEAF_ROWS ** -0.5, 0.1875, ((0, 128),), jnp.float32)
    leaf_back = gaussian(streams_of[3], (N_LEAF * LEAF_ROWS, LOW_RANK), LOW_RANK ** -0.5, 0.375, ((0, 128),), jnp.float32)
    level_one = gaussian(streams_of[4], (N_LEAF * LOW_RANK, 4 * LOW_RANK), (2 * LOW_RANK) ** -0.5, 0.25, ((0, 128),), jnp.float32)
    level_two = gaussian(streams_of[5], (N_LEAF * LOW_RANK // 2, 4 * LOW_RANK), (2 * LOW_RANK) ** -0.5, 0.25, ((0, 128),), jnp.float32)
    level_three = gaussian(streams_of[6], (N_LEAF * LOW_RANK // 4, 4 * LOW_RANK), (2 * LOW_RANK) ** -0.5, 0.25, ((0, 128),), jnp.float32)
    top_inverse = draw_top_inverse(jax.random.fold_in(streams_of[8], 71), 0)
    return {"shots": shots, "leaf_inverse": leaf_inverse, "leaf_basis": leaf_basis, "leaf_back": leaf_back, "level_one": level_one, "level_two": level_two, "level_three": level_three, "top_inverse": top_inverse}


def reference(shots, leaf_inverse, leaf_basis, leaf_back, level_one, level_two, level_three, top_inverse):
    highest = lax.Precision.HIGHEST
    leaves = N_LEAF
    rhs_blocks = shots.reshape(leaves, LEAF_ROWS, SHOT_COUNT)
    eliminators = leaf_inverse.reshape(leaves, LEAF_ROWS, LEAF_ROWS)
    solved = jnp.einsum("nij,njs->nis", eliminators, rhs_blocks, precision=highest)
    bases = leaf_basis.reshape(leaves, LOW_RANK, LEAF_ROWS)
    reduced = jnp.einsum("nrm,nms->nrs", bases, solved, precision=highest)
    stored = []
    for factors in (level_one, level_two, level_three):
        nodes = reduced.shape[0] // 2
        blocks = factors.reshape(nodes, 2 * LOW_RANK, 4 * LOW_RANK)
        inverse_block = blocks[:, :, :2 * LOW_RANK]
        reduce_block = blocks[:, :, 2 * LOW_RANK:3 * LOW_RANK]
        back_block = blocks[:, :, 3 * LOW_RANK:]
        stacked = reduced.reshape(nodes, 2 * LOW_RANK, SHOT_COUNT)
        coupled = jnp.einsum("nij,njs->nis", inverse_block, stacked, precision=highest)
        reduced = jnp.einsum("nir,nis->nrs", reduce_block, coupled, precision=highest)
        stored.append((coupled, back_block))
    gathered = reduced.reshape(TOP_NODES * LOW_RANK, SHOT_COUNT)
    top_solution = jnp.dot(top_inverse, gathered, precision=highest)
    coefficient = top_solution.reshape(TOP_NODES, LOW_RANK, SHOT_COUNT)
    for coupled, back_block in reversed(stored):
        remainder = coupled - jnp.einsum("nir,nrs->nis", back_block, coefficient, precision=highest)
        coefficient = remainder.reshape(-1, LOW_RANK, SHOT_COUNT)
    backs = leaf_back.reshape(leaves, LEAF_ROWS, LOW_RANK)
    result = solved - jnp.einsum("nmr,nrs->nms", backs, coefficient, precision=highest)
    return result.reshape(leaves * LEAF_ROWS, SHOT_COUNT)
```

```python
import functools

import jax
import jax.numpy as jnp
from jax import lax
from jax.experimental import pallas as pl
from jax.experimental.pallas import tpu as pltpu
from jax.sharding import PartitionSpec as P

CORE, X_NEAR, X_FAR = 1, 2, 6
RINGS = (8, 32, 24, 96)
BLOCKS = 8
TREE = 8


def swap(value, mask):
    return lax.ppermute(value, "leaf", [(i, i ^ mask) for i in range(lax.axis_size("leaf"))])


def dot(a, b):
    return jnp.dot(a, b, precision=lax.Precision.HIGH)


def dot_rows(a, b):
    return lax.dot_general(a, b, (((0,), (0,)), ((), ())), precision=lax.Precision.HIGH)


def halves(value):
    high = value.astype(jnp.bfloat16)
    return high, (value - high.astype(jnp.float32)).astype(jnp.bfloat16)


def product(a_high, a_low, b_high, b_low):
    part = functools.partial(jnp.dot, preferred_element_type=jnp.float32)
    return part(a_high, b_high) + (part(a_high, b_low) + part(a_low, b_high))


def call(body, grid, in_specs, out_specs, out_shape, scratch, flops, moved):
    return pl.pallas_call(
        body,
        grid_spec=pltpu.PrefetchScalarGridSpec(
            num_scalar_prefetch=1,
            grid=grid,
            in_specs=in_specs,
            out_specs=out_specs,
            scratch_shapes=scratch,
        ),
        out_shape=out_shape,
        compiler_params=pltpu.CompilerParams(vmem_limit_bytes=40 * 2**20),
        cost_estimate=pl.CostEstimate(flops=flops, bytes_accessed=moved, transcendentals=0),
    )


def reduce_body(base, basis, inverse, shots, out, high, low):
    @pl.when(pl.program_id(0) == 0)
    def _():
        high[...], low[...] = halves(product(*halves(basis[...]), *halves(inverse[...])))

    out[...] = product(high[...], low[...], *halves(shots[...]))


def reduce_leaf(base, basis, inverse, shots):
    rank, rows = basis.shape
    width = shots.shape[1] // BLOCKS
    return call(
        reduce_body,
        (BLOCKS,),
        [
            pl.BlockSpec((rank, rows), lambda p, base: (0, 0)),
            pl.BlockSpec((rows, rows), lambda p, base: (0, 0)),
            pl.BlockSpec((rows, width), lambda p, base: (0, base[0] ^ p)),
        ],
        pl.BlockSpec((rank, width), lambda p, base: (0, p)),
        jax.ShapeDtypeStruct((rank, shots.shape[1]), jnp.float32),
        [pltpu.VMEM((rank, rows), jnp.bfloat16), pltpu.VMEM((rank, rows), jnp.bfloat16)],
        6 * rank * rows * (rows + shots.shape[1]),
        4 * (rows * rows + rows * shots.shape[1]),
    )(base, basis, inverse, shots)


def leaf_body(base, inverse, shots, out, high, low):
    @pl.when(pl.program_id(0) == 0)
    def _():
        high[...], low[...] = halves(inverse[...])

    out[...] = product(high[...], low[...], *halves(shots[...]))


def solve_leaf(base, inverse, shots, first, count):
    rows = inverse.shape[0]
    width = shots.shape[1] // BLOCKS
    return call(
        leaf_body,
        (count,),
        [
            pl.BlockSpec((rows, rows), lambda p, base: (0, 0)),
            pl.BlockSpec((rows, width), lambda p, base: (0, base[0] ^ (p + first))),
        ],
        pl.BlockSpec((rows, width), lambda p, base: (0, p)),
        jax.ShapeDtypeStruct((rows, count * width), jnp.float32),
        [pltpu.VMEM((rows, rows), jnp.bfloat16), pltpu.VMEM((rows, rows), jnp.bfloat16)],
        6 * rows * rows * count * width,
        4 * (rows * rows + 2 * rows * count * width),
    )(base, inverse, shots)


def finish_body(base, back, own, other, near, far, out, high, low):
    p = pl.program_id(0)
    half = pl.num_programs(0) // 2

    @pl.when(p == 0)
    def _():
        high[...], low[...] = halves(back[...])

    @pl.when(p < half)
    def _():
        out[...] = near[...] - product(high[...], low[...], *halves(own[...]))

    @pl.when(p >= half)
    def _():
        out[...] = far[...] - product(high[...], low[...], *halves(other[...]))


def finish(base, back, own, other, near, far):
    rows, rank = back.shape
    half = BLOCKS // 2
    width = own.shape[1] // half
    first = lambda p, base: (0, jnp.minimum(p, half - 1))
    second = lambda p, base: (0, jnp.maximum(p - half, 0))
    return call(
        finish_body,
        (BLOCKS,),
        [
            pl.BlockSpec((rows, rank), lambda p, base: (0, 0)),
            pl.BlockSpec((rank, width), first),
            pl.BlockSpec((rank, width), second),
            pl.BlockSpec((rows, width), first),
            pl.BlockSpec((rows, width), second),
        ],
        pl.BlockSpec((rows, width), lambda p, base: (0, base[0] ^ p)),
        jax.ShapeDtypeStruct((rows, BLOCKS * width), jnp.float32),
        [pltpu.VMEM((rows, rank), jnp.bfloat16), pltpu.VMEM((rows, rank), jnp.bfloat16)],
        6 * rows * rank * BLOCKS * width,
        4 * 2 * rows * BLOCKS * width,
    )(base, back, own, other, near, far)


def top_body(places, node, inverse, *rest):
    pieces, (out, high, low) = rest[:-3], rest[-3:]
    rows, width = pieces[0].shape
    for piece, (row, column, nodes) in zip(pieces, places):
        for at, mask in enumerate(nodes):
            start = pl.multiple_of((node[0] ^ mask) * 2 * rows + row * rows, rows)
            part = halves(piece[at * rows : (at + 1) * rows, :])
            high[pl.ds(start, rows), column * width : (column + 1) * width] = part[0]
            low[pl.ds(start, rows), column * width : (column + 1) * width] = part[1]
    out[...] = product(*halves(inverse[...]), high[...], low[...])


def solve_top(node, inverse, pieces, places):
    rank, order = inverse.shape
    width = 2 * pieces[0].shape[1]
    whole = lambda value: pl.BlockSpec(value.shape, lambda p, node: (0, 0))
    return call(
        functools.partial(top_body, places),
        (1,),
        [whole(inverse)] + [whole(piece) for piece in pieces],
        pl.BlockSpec((rank, width), lambda p, node: (0, 0)),
        jax.ShapeDtypeStruct((rank, width), jnp.float32),
        [pltpu.VMEM((order, width), jnp.bfloat16), pltpu.VMEM((order, width), jnp.bfloat16)],
        6 * rank * order * width,
        4 * order * (rank + width),
    )(node, inverse, *pieces)


def spread_top(reduced):
    rows, width = reduced.shape[0] // 2, reduced.shape[1] // 2
    held, order = [], [[0] for _ in RINGS]
    for quarter in range(len(RINGS)):
        row, column = divmod(quarter, 2)
        held.append([reduced[row * rows : (row + 1) * rows, column * width : (column + 1) * width]])
    for step in range(len(RINGS)):
        ways = [RINGS[(quarter + step) % len(RINGS)] for quarter in range(len(RINGS))]
        sent = [jnp.concatenate(parts, 0) if step else parts[0] for parts in held]
        arrived = [swap(value, way) for value, way in zip(sent, ways)]
        for quarter, way in enumerate(ways):
            held[quarter].append(arrived[quarter])
            order[quarter] += [mask ^ way for mask in order[quarter]]
    pieces, places = [], []
    for quarter, parts in enumerate(held):
        row, column = divmod(quarter, 2)
        at = 0
        for part in parts:
            count = part.shape[0] // rows
            pieces.append(part)
            places.append((row, column, [mask // TREE for mask in order[quarter][at : at + count]]))
            at += count
    return pieces, places


def own_first(value, second, axis):
    size = value.shape[axis] // 2
    low, high = jnp.split(value, 2, axis)
    return jnp.concatenate([jnp.where(second, high, low), jnp.where(second, low, high)], axis)


def node_blocks(factors, second, rank):
    inverse = own_first(factors[:, : 2 * rank], second, 1)
    return inverse, dot_rows(factors[:, 2 * rank : 3 * rank], inverse), factors[:, 3 * rank :]


def shards(
    shots, leaf_inverse, leaf_basis, leaf_back, level_one, level_two, level_three, top_inverse
):
    rank = leaf_basis.shape[0]
    place = lax.axis_index("leaf")
    core, near, far = place & 1, place >> 1 & 1, place >> 2 & 1
    base = jnp.reshape(core << 2 | (near ^ far) << 1 | far, (1,)).astype(jnp.int32)
    node = jnp.reshape(place // TREE, (1,)).astype(jnp.int32)
    groups = [list(range(i, i + TREE)) for i in range(0, lax.axis_size("leaf"), TREE)]
    gather = functools.partial(
        lax.all_gather, axis_name="leaf", axis_index_groups=groups, axis=0, tiled=True
    )

    three = own_first(gather(level_three), far == 1, 0)
    top_rows = gather(top_inverse)
    two_beside = swap(level_two, X_NEAR)
    one = jnp.concatenate([level_one, swap(level_one, CORE)], 0)
    two_own = jnp.concatenate([level_two, two_beside], 1)
    two_other = swap(two_own, CORE)
    two = jnp.where(
        core == 1,
        jnp.concatenate([two_other, two_own], 0),
        jnp.concatenate([two_own, two_other], 0),
    )
    two = jnp.concatenate(jnp.split(two, 2, 1), 0)
    inverse_1, down_1, back_1 = node_blocks(one, core == 1, rank)
    inverse_2, down_2, back_2 = node_blocks(two, near == 1, rank)
    inverse_3, down_3, back_3 = node_blocks(three, far == 1, rank)

    reduced = reduce_leaf(base, leaf_basis, leaf_inverse, shots)
    size = reduced.shape[1] // 2
    pair = jnp.concatenate([reduced[:, :size], swap(reduced[:, size:], CORE)], 0)
    reduced = dot(down_1, pair)
    coupled_1 = dot(inverse_1, pair)
    size //= 2
    pair = jnp.concatenate([reduced[:, :size], swap(reduced[:, size:], X_NEAR)], 0)
    reduced = dot(down_2, pair)
    coupled_2 = dot(inverse_2, pair)
    size //= 2
    pair = jnp.concatenate([reduced[:, :size], swap(reduced[:, size:], X_FAR)], 0)
    reduced = dot(down_3, pair)
    coupled_3 = dot(inverse_3, pair)

    solved_near = solve_leaf(base, leaf_inverse, shots, 0, BLOCKS // 2)
    solved_far = solve_leaf(base, leaf_inverse, shots, BLOCKS // 2, BLOCKS // 2)

    pieces, places = spread_top(reduced)
    coefficient = solve_top(node, top_rows, pieces, places)
    for coupled, back, mask in ((coupled_3, back_3, X_FAR), (coupled_2, back_2, X_NEAR)):
        other = swap(coupled[rank:] - dot(back[rank:], coefficient), mask)
        own = coupled[:rank] - dot(back[:rank], coefficient)
        coefficient = jnp.concatenate([own, other], 1)
    other = swap(coupled_1[rank:] - dot(back_1[rank:], coefficient), CORE)
    own = coupled_1[:rank] - dot(back_1[:rank], coefficient)
    return finish(base, leaf_back, own, other, solved_near, solved_far)


def solution(mesh):
    return jax.shard_map(
        shards,
        mesh=mesh,
        in_specs=(P("leaf", None),) * 8,
        out_specs=P("leaf", None),
        check_vma=False,
    )
```

```python
import functools
import math

import jax
import jax.numpy as jnp
from jax import lax
from jax.experimental import pallas as pl
from jax.experimental.pallas import tpu as pltpu
from jax.sharding import PartitionSpec as P

CORE, X_NEAR, X_FAR = 1, 2, 6
RINGS = (8, 32, 24, 96)
BLOCKS = 8
TREE = 8


def swap(value, mask):
    return lax.ppermute(value, "leaf", [(i, i ^ mask) for i in range(lax.axis_size("leaf"))])


ROW_STEPS = 4
SPARE_BYTES = 6 * 2**20


def after(values, ready):
    return lax.optimization_barrier((values, ready))[0]


def halves(value):
    high = value.astype(jnp.bfloat16)
    return high, (value - high.astype(jnp.float32)).astype(jnp.bfloat16)


part = functools.partial(jnp.dot, preferred_element_type=jnp.float32)


def product(a_high, a_low, b):
    b_high, b_low = halves(b)
    return part(a_high, b_high) + (part(a_high, b_low) + part(a_low, b_high))


def pair_product(a_high, a_low, own, other):
    rank = own.shape[0]
    return product(a_high[:, :rank], a_low[:, :rank], own) + product(
        a_high[:, rank:], a_low[:, rank:], other
    )


def call(body, grid, scalars, operands, results, scratch, flops, aliases=None):
    zero = lambda p, s: (0, 0)
    full = lambda item: item if isinstance(item, tuple) else (item, item.shape, zero)
    operands, results = [full(item) for item in operands], [full(item) for item in results]
    spec = lambda item: pl.BlockSpec(memory_space=pl.ANY) if item[1] is None else pl.BlockSpec(item[1], item[2])
    held = 2 * sum(math.prod(item[1]) * item[0].dtype.itemsize for item in operands + results if item[1])
    held += sum(math.prod(item.shape) * jnp.dtype(item.dtype).itemsize for item in scratch)
    moved = sum(4 * math.prod(item[0].shape) for item in operands + results)
    return pl.pallas_call(
        body,
        grid_spec=pltpu.PrefetchScalarGridSpec(
            num_scalar_prefetch=1,
            grid=(grid,),
            in_specs=[spec(item) for item in operands],
            out_specs=[spec(item) for item in results],
            scratch_shapes=scratch,
        ),
        out_shape=[item[0] for item in results],
        input_output_aliases=aliases or {},
        compiler_params=pltpu.CompilerParams(vmem_limit_bytes=held + SPARE_BYTES),
        cost_estimate=pl.CostEstimate(flops=flops, bytes_accessed=moved if flops else 0, transcendentals=0),
    )(scalars, *[item[0] for item in operands])


def f32(*shape):
    return jax.ShapeDtypeStruct(shape, jnp.float32)


def hbm(value):
    return pltpu.with_memory_space_constraint(value, pltpu.HBM)


def both(*shape, space=jax.ShapeDtypeStruct):
    return [space(shape, jnp.bfloat16)] * 2


def lead_body(base, basis, inverse, shots, high, low, *pieces):
    p = pl.program_id(0)

    @pl.when(p == 0)
    def _():
        high[...], low[...] = halves(product(*halves(basis[...]), inverse[...]))

    reduced = product(high[...], low[...], shots[...])
    for i, piece in enumerate(pieces):

        @pl.when(p == i)
        def _():
            piece[...] = reduced


def reduce_lead(base, basis, inverse, shots):
    rank, rows = basis.shape
    width, half = shots.shape[1] // BLOCKS, BLOCKS // 2
    return call(
        lead_body,
        half,
        base,
        [basis, hbm(inverse), (hbm(shots), (rows, width), lambda p, base: (0, base[0] ^ (p + half)))],
        both(rank, rows) + [f32(rank, width)] * half,
        [],
        6 * rank * rows * (rows + half * width),
    )


def reduce_body(base, high, low, shots, out):
    out[...] = product(high[...], low[...], shots[...])


def reduce_own(base, high, low, shots):
    rank, rows = high.shape
    width, half = shots.shape[1] // BLOCKS, BLOCKS // 2
    return call(
        reduce_body,
        half,
        base,
        [high, low, (hbm(shots), (rows, width), lambda p, base: (0, base[0] ^ p))],
        [(f32(rank, half * width), (rank, width), lambda p, base: (0, p))],
        [],
        6 * rank * rows * half * width,
    )[0]


def leaf_body(half, inverse, shots, out, high, low):
    @pl.when(pl.program_id(0) == 0)
    def _():
        high[...], low[...] = halves(shots[...])

    a_high, a_low = halves(inverse[...])
    out[...] = part(a_high, high[...]) + (part(a_high, low[...]) + part(a_low, high[...]))


def solve_leaf(half, inverse, shots, space):
    rows = inverse.shape[0]
    width, unit = shots.shape[1] // 2, rows // ROW_STEPS
    return call(
        leaf_body,
        ROW_STEPS,
        half,
        [(hbm(inverse), (unit, rows), lambda p, half: (p, 0)), (hbm(shots), (rows, width), lambda p, half: (0, half[0]))],
        [(space((rows, width), jnp.float32), (unit, width), lambda p, half: (p, 0))],
        [pltpu.VMEM((rows, width), jnp.bfloat16)] * 2,
        6 * rows * rows * width,
    )[0]


def finish_body(at, back, coefficient, solved, *rest):
    out, high, low = rest[-3:]

    @pl.when(pl.program_id(0) == 0)
    def _():
        width = coefficient.shape[1] * 2 // BLOCKS
        for p in range(BLOCKS // 2):
            columns = pl.ds(pl.multiple_of((at[1] ^ p) * width, width), width)
            high[:, columns], low[:, columns] = halves(coefficient[:, p * width : (p + 1) * width])

    a_high, a_low = halves(back[...])
    out[...] = solved[...] - (
        part(a_high, high[...]) + (part(a_high, low[...]) + part(a_low, high[...]))
    )


def finish(at, back, coefficient, solved, total):
    rows, rank = back.shape
    width, unit = solved.shape[1], rows // ROW_STEPS
    return call(
        finish_body,
        ROW_STEPS,
        at,
        [
            (back, (unit, rank), lambda p, at: (p, 0)),
            coefficient,
            (solved, (unit, width), lambda p, at: (p, 0)),
        ]
        + ([] if total is None else [(total, None, None)]),
        [(pltpu.HBM((rows, 2 * width), jnp.float32), (unit, width), lambda p, at: (p, at[0]))],
        [pltpu.VMEM((rank, width), jnp.bfloat16)] * 2,
        6 * rows * rank * width,
        {} if total is None else {4: 0},
    )[0]


def node_body(count, units, at, *refs):
    pieces = refs[:count]
    down_high, down_low, high, low, back_high, back_low, factors = refs[count:]
    rank = down_high.shape[0]
    unit = factors.shape[0] // units
    done = 0
    for piece in pieces:
        for k in range(piece.shape[0] // unit):
            start = pl.multiple_of(at[done + 1], unit)
            factors[pl.ds(start, unit), :] = piece[k * unit : (k + 1) * unit, :]
            done += 1
    for i, child in enumerate((at[0], 1 - at[0])):
        columns = slice(i * rank, (i + 1) * rank)
        block = factors[:, pl.ds(pl.multiple_of(child * rank, rank), rank)]
        high[:, columns], low[:, columns] = halves(block)
    lead_high, lead_low = halves(factors[:, 2 * rank : 3 * rank].T)
    back_high[...], back_low[...] = halves(factors[:, 3 * rank :])
    down = part(lead_high, high[...]) + (
        part(lead_high, low[...]) + part(lead_low, high[...])
    )
    down_high[...], down_low[...] = halves(down)


def node_blocks(pieces, starts, second, rank):
    at = jnp.stack([second] + starts).astype(jnp.int32)
    results = call(
        functools.partial(node_body, len(pieces), len(starts)),
        1,
        at,
        pieces,
        both(rank, 2 * rank)
        + both(2 * rank, 2 * rank, space=pltpu.HBM)
        + both(2 * rank, rank, space=pltpu.HBM),
        [pltpu.VMEM((2 * rank, 4 * rank), jnp.float32)],
        6 * rank * 4 * rank * rank,
    )
    return results[:2], results[2:4], results[4:]


def pair_body(base, high, low, own, *rest):
    pieces, results = rest[:-2], rest[-2:]
    held, width = pieces[0].shape[1], min(pieces[0].shape[1], results[0].shape[1])
    at = 0
    for result in results[::-1]:
        for start in range(0, result.shape[1], width):
            piece = pieces[at // held][:, at % held : at % held + width]
            result[:, start : start + width] = pair_product(
                high[...], low[...], own[:, at : at + width], piece
            )
            at += width


def reduce_pair(base, down, own, pieces):
    rank, size = own.shape
    return call(
        pair_body,
        1,
        base,
        [*down, own, *pieces],
        [f32(rank, size // 2)] * 2,
        [],
        12 * rank * rank * size,
    )


def couple_body(base, high, low, own, *rest):
    pieces, out = rest[:-1], rest[-1]
    width = pieces[0].shape[1]
    for i, piece in enumerate(pieces):
        columns = slice(i * width, (i + 1) * width)
        out[:, columns] = pair_product(high[...], low[...], own[:, columns], piece[...])


def couple(base, inverse, own, pieces):
    rank, size = own.shape
    return call(
        couple_body, 1, base, [*inverse, own, *pieces], [pltpu.HBM((2 * rank, size), jnp.float32)], [], 24 * rank * rank * size
    )[0]


def quarter_body(base, high, low, own, other, *quarters):
    reduced = pair_product(high[...], low[...], own[...], other[...])
    rows, width = quarters[0].shape
    for i, quarter in enumerate(quarters):
        row, column = divmod(i, 2)
        quarter[...] = reduced[row * rows : (row + 1) * rows, column * width : (column + 1) * width]


def reduce_quarters(base, down, own, other):
    rank, size = own.shape
    return call(
        quarter_body,
        1,
        base,
        [*down, own, other],
        [f32(rank // 2, size // 2)] * len(RINGS),
        [],
        12 * rank * rank * size,
    )


def back_body(base, high, low, coupled, *rest):
    coefficients, out = rest[:-1], rest[-1]
    at = 0
    for coefficient in coefficients:
        columns = slice(at, at + coefficient.shape[1])
        out[:, columns] = coupled[:, columns] - product(high[...], low[...], coefficient[...])
        at += coefficient.shape[1]


def back_substitute(base, back, coupled, coefficients, child):
    rank = back[0].shape[1]
    size = coupled.shape[1]
    rows = lambda p, base: (child, 0)
    return call(
        back_body,
        1,
        base,
        [(back[0], (rank, rank), rows), (back[1], (rank, rank), rows), (coupled, (rank, size), rows), *coefficients],
        [f32(rank, size)],
        [],
        6 * rank * rank * size,
    )[0]


def split_body(node, value, high, low):
    high[...], low[...] = halves(value[...])


def top_body(places, node, high, low, *rest):
    pieces, (out, c_high, c_low) = rest[:-3], rest[-3:]
    rows, width = pieces[0].shape
    for piece, (row, column, nodes) in zip(pieces, places):
        for at, mask in enumerate(nodes):
            start = pl.multiple_of((node[0] ^ mask) * 2 * rows + row * rows, rows)
            block = halves(piece[at * rows : (at + 1) * rows, :])
            columns = slice(column * width, (column + 1) * width)
            c_high[pl.ds(start, rows), columns], c_low[pl.ds(start, rows), columns] = block
    out[...] = part(high[...], c_high[...]) + (
        part(high[...], c_low[...]) + part(low[...], c_high[...])
    )


def solve_top(node, inverse, pieces, places):
    rank, order = inverse[0].shape
    width = 2 * pieces[0].shape[1]
    return call(
        functools.partial(top_body, places),
        1,
        node,
        [*inverse, *pieces],
        [f32(rank, width)],
        [pltpu.VMEM((order, width), jnp.bfloat16)] * 2,
        6 * rank * order * width,
    )[0]


def shards(
    shots, leaf_inverse, leaf_basis, leaf_back, level_one, level_two, level_three, top_inverse
):
    rank = leaf_basis.shape[0]
    place = lax.axis_index("leaf")
    core, near, far = place & 1, place >> 1 & 1, place >> 2 & 1
    base = jnp.reshape(core << 2 | (near ^ far) << 1 | far, (1,)).astype(jnp.int32)
    node = jnp.reshape(place // TREE, (1,)).astype(jnp.int32)

    half = jnp.stack([core, base[0] & 3]).astype(jnp.int32)
    other_half = jnp.stack([1 - core, base[0] & 3]).astype(jnp.int32)

    groups = [list(range(i, i + TREE)) for i in range(0, lax.axis_size("leaf"), TREE)]
    gather = functools.partial(
        lax.all_gather, axis_name="leaf", axis_index_groups=groups, axis=0, tiled=True
    )
    one_other = swap(level_one, CORE)
    two_near = swap(level_two, X_NEAR)
    three_near, three_far = swap(level_three, X_NEAR), swap(level_three, X_FAR)

    high, low, *sent = reduce_lead(base, leaf_basis, leaf_inverse, shots)
    other = [swap(piece, CORE) for piece in sent]
    own = reduce_own(base, high, low, shots)
    down_1, inverse_1, back_1 = node_blocks(
        [level_one, one_other], [0 * core, 0 * core + rank], core, rank
    )
    own, two_near, three_near, three_far = lax.optimization_barrier(
        (own, two_near, three_near, three_far)
    )
    sent, own_1 = reduce_pair(base, down_1, own, other)
    other_1 = swap(sent, X_NEAR)
    solved = [solve_leaf(half, leaf_inverse, after(shots, sent), pltpu.HBM)]
    three_near = after(three_near, sent)
    three_both = swap(three_near, X_FAR)
    other_1, three_both, solved[0] = lax.optimization_barrier((other_1, three_both, solved[0]))

    rows_2, rows_3 = level_two.shape[0], level_three.shape[0]
    two = [level_two, swap(level_two, CORE), two_near, swap(two_near, CORE)]
    starts = [core * rows_2, (1 - core) * rows_2]
    down_2, inverse_2, back_2 = node_blocks(
        two, starts + [rank + start for start in starts], near, rank
    )
    sent, own_2 = reduce_pair(base, down_2, own_1, [other_1])
    other_2 = swap(sent, X_FAR)
    top = gather(after(top_inverse, sent))
    own, other, own_1, other_1 = after((own, other, own_1, other_1), sent)
    coupled_1 = couple(base, inverse_1, own, other)
    coupled_2 = couple(base, inverse_2, own_1, [other_1])
    three = [level_three, three_near, three_far, three_both]
    three += [swap(value, CORE) for value in three]
    starts = []
    for flip in (0, X_FAR, CORE, X_FAR | CORE):
        for mask in (0, X_NEAR):
            seat = place ^ mask ^ flip
            starts.append(((seat ^ far << 2) >> 2 & 1) * rank + (seat & 3) * rows_3)
    down_3, inverse_3, back_3 = node_blocks(three, starts, far, rank)
    quarters = reduce_quarters(base, down_3, own_2, other_2)

    held, order = [[quarter] for quarter in quarters], [[0] for _ in RINGS]
    for step in range(len(RINGS)):
        sent = [jnp.concatenate(parts, 0) if step else parts[0] for parts in held]
        if step == len(RINGS) - 1:
            sent[-1], top = lax.optimization_barrier((sent[-1], top))
        for quarter in range(len(RINGS)):
            way = RINGS[(quarter + step) % len(RINGS)]
            held[quarter].append(swap(sent[quarter], way))
            order[quarter] += [mask ^ way for mask in order[quarter]]
        if step == 0:
            coupled_3 = couple(base, inverse_3, own_2, [other_2])
    unit = rank // ROW_STEPS
    block = ((unit, top.shape[1]), lambda p, node: (p, 0))
    top_rows = call(
        split_body,
        ROW_STEPS,
        node,
        [(hbm(top), *block)],
        [(value, *block) for value in both(*top.shape)],
        [],
        rank * top.shape[1],
    )
    pieces, places = [], []
    for quarter, parts in enumerate(held):
        row, column = divmod(quarter, 2)
        at = 0
        for value in parts:
            count = value.shape[0] // (rank // 2)
            pieces.append(value)
            places.append((row, column, [mask // TREE for mask in order[quarter][at : at + count]]))
            at += count
    coefficients = [solve_top(node, top_rows, pieces, places)]
    levels = ((coupled_3, back_3, X_FAR), (coupled_2, back_2, X_NEAR), (coupled_1, back_1, CORE))
    for coupled, back, mask in levels:
        sent = back_substitute(base, back, coupled, coefficients, 1)
        other = swap(sent, mask)
        own = back_substitute(base, back, coupled, coefficients, 0)
        if mask == X_NEAR:
            solved.append(solve_leaf(other_half, leaf_inverse, after(shots, sent), jax.ShapeDtypeStruct))
            other, solved[1] = lax.optimization_barrier((other, solved[1]))
        coefficients = [own, other]
    total = finish(half, leaf_back, own, solved[0], None)
    return finish(other_half, leaf_back, other, solved[1], total)


def solution(mesh):
    return jax.shard_map(
        shards,
        mesh=mesh,
        in_specs=(P("leaf", None),) * 8,
        out_specs=P("leaf", None),
        check_vma=False,
    )
```

```python
import functools
import math

import jax
import jax.numpy as jnp
from jax import lax
from jax.experimental import pallas as pl
from jax.experimental.pallas import tpu as pltpu
from jax.sharding import PartitionSpec as P

CORE, X_NEAR, X_FAR = 1, 2, 6
RINGS = (8, 32, 24, 96)
BLOCKS = 8
TREE = 8


def swap(value, mask):
    return lax.ppermute(value, "leaf", [(i, i ^ mask) for i in range(lax.axis_size("leaf"))])


ROW_STEPS = 4
SPARE_BYTES = 6 * 2**20


def after(values, ready):
    return lax.optimization_barrier((values, ready))[0]


def halves(value):
    high = value.astype(jnp.bfloat16)
    return high, (value - high.astype(jnp.float32)).astype(jnp.bfloat16)


part = functools.partial(jnp.dot, preferred_element_type=jnp.float32)


def product(a_high, a_low, b):
    b_high, b_low = halves(b)
    return part(a_high, b_high) + (part(a_high, b_low) + part(a_low, b_high))


def pair_product(a_high, a_low, own, other):
    rank = own.shape[0]
    return product(a_high[:, :rank], a_low[:, :rank], own) + product(
        a_high[:, rank:], a_low[:, rank:], other
    )


def call(body, grid, scalars, operands, results, scratch, flops, aliases=None):
    zero = lambda p, s: (0, 0)
    full = lambda item: item if isinstance(item, tuple) else (item, item.shape, zero)
    operands, results = [full(item) for item in operands], [full(item) for item in results]
    spec = lambda item: pl.BlockSpec(memory_space=pl.ANY) if item[1] is None else pl.BlockSpec(item[1], item[2])
    held = 2 * sum(math.prod(item[1]) * item[0].dtype.itemsize for item in operands + results if item[1])
    held += sum(math.prod(item.shape) * jnp.dtype(item.dtype).itemsize for item in scratch)
    moved = sum(4 * math.prod(item[0].shape) for item in operands + results)
    return pl.pallas_call(
        body,
        grid_spec=pltpu.PrefetchScalarGridSpec(
            num_scalar_prefetch=1,
            grid=(grid,),
            in_specs=[spec(item) for item in operands],
            out_specs=[spec(item) for item in results],
            scratch_shapes=scratch,
        ),
        out_shape=[item[0] for item in results],
        input_output_aliases=aliases or {},
        compiler_params=pltpu.CompilerParams(vmem_limit_bytes=held + SPARE_BYTES),
        cost_estimate=pl.CostEstimate(flops=flops, bytes_accessed=moved if flops else 0, transcendentals=0),
    )(scalars, *[item[0] for item in operands])


def f32(*shape):
    return jax.ShapeDtypeStruct(shape, jnp.float32)


def hbm(value):
    return pltpu.with_memory_space_constraint(value, pltpu.HBM)


def both(*shape, space=jax.ShapeDtypeStruct):
    return [space(shape, jnp.bfloat16)] * 2


def reduce_body(base, basis, inverse, shots, *refs):
    pieces, (own, high, low) = refs[:-3], refs[-3:]
    p = pl.program_id(0)

    @pl.when(p == 0)
    def _():
        high[...], low[...] = halves(product(*halves(basis[...]), inverse[...]))

    reduced = product(high[...], low[...], shots[...])
    for i, piece in enumerate(pieces):

        @pl.when(p == i)
        def _():
            piece[...] = reduced

    @pl.when(p >= len(pieces))
    def _():
        own[...] = reduced


def reduce_leaf(base, basis, inverse, shots):
    rank, rows = basis.shape
    width, half = shots.shape[1] // BLOCKS, BLOCKS // 2
    return call(
        reduce_body,
        BLOCKS,
        base,
        [hbm(basis), hbm(inverse), (hbm(shots), (rows, width), lambda p, base: (0, base[0] ^ (p + half) % BLOCKS))],
        [f32(rank, width)] * half
        + [
            (
                pltpu.HBM((rank, half * width), jnp.float32),
                (rank, width),
                lambda p, base: (0, jnp.maximum(p - half, 0)),
            )
        ],
        [pltpu.VMEM((rank, rows), jnp.bfloat16)] * 2,
        6 * rank * rows * (rows + shots.shape[1]),
    )


def leaf_body(half, inverse, shots, out, high, low):
    @pl.when(pl.program_id(0) == 0)
    def _():
        high[...], low[...] = halves(shots[...])

    a_high, a_low = halves(inverse[...])
    out[...] = part(a_high, high[...]) + (part(a_high, low[...]) + part(a_low, high[...]))


def solve_leaf(half, inverse, shots, space):
    rows = inverse.shape[0]
    width, unit = shots.shape[1] // 2, rows // ROW_STEPS
    return call(
        leaf_body,
        ROW_STEPS,
        half,
        [(hbm(inverse), (unit, rows), lambda p, half: (p, 0)), (hbm(shots), (rows, width), lambda p, half: (0, half[0]))],
        [(space((rows, width), jnp.float32), (unit, width), lambda p, half: (p, 0))],
        [pltpu.VMEM((rows, width), jnp.bfloat16)] * 2,
        6 * rows * rows * width,
    )[0]


def finish_body(at, back, coefficient, solved, *rest):
    out, high, low = rest[-3:]

    @pl.when(pl.program_id(0) == 0)
    def _():
        width = coefficient.shape[1] * 2 // BLOCKS
        for p in range(BLOCKS // 2):
            columns = pl.ds(pl.multiple_of((at[1] ^ p) * width, width), width)
            high[:, columns], low[:, columns] = halves(coefficient[:, p * width : (p + 1) * width])

    a_high, a_low = halves(back[...])
    out[...] = solved[...] - (
        part(a_high, high[...]) + (part(a_high, low[...]) + part(a_low, high[...]))
    )


def finish(at, back, coefficient, solved, total):
    rows, rank = back.shape
    width, unit = solved.shape[1], rows // ROW_STEPS
    return call(
        finish_body,
        ROW_STEPS,
        at,
        [
            (back, (unit, rank), lambda p, at: (p, 0)),
            coefficient,
            (solved, (unit, width), lambda p, at: (p, 0)),
        ]
        + ([] if total is None else [(total, None, None)]),
        [(pltpu.HBM((rows, 2 * width), jnp.float32), (unit, width), lambda p, at: (p, at[0]))],
        [pltpu.VMEM((rank, width), jnp.bfloat16)] * 2,
        6 * rows * rank * width,
        {} if total is None else {4: 0},
    )[0]


def node_body(count, units, at, *refs):
    pieces = refs[:count]
    down_high, down_low, high, low, back_high, back_low, factors = refs[count:]
    rank = down_high.shape[0]
    unit = factors.shape[0] // units
    done = 0
    for piece in pieces:
        for k in range(piece.shape[0] // unit):
            start = pl.multiple_of(at[done + 1], unit)
            factors[pl.ds(start, unit), :] = piece[k * unit : (k + 1) * unit, :]
            done += 1
    for i, child in enumerate((at[0], 1 - at[0])):
        columns = slice(i * rank, (i + 1) * rank)
        block = factors[:, pl.ds(pl.multiple_of(child * rank, rank), rank)]
        high[:, columns], low[:, columns] = halves(block)
    lead_high, lead_low = halves(factors[:, 2 * rank : 3 * rank].T)
    back_high[...], back_low[...] = halves(factors[:, 3 * rank :])
    down = part(lead_high, high[...]) + (
        part(lead_high, low[...]) + part(lead_low, high[...])
    )
    down_high[...], down_low[...] = halves(down)


def node_blocks(pieces, starts, second, rank):
    at = jnp.stack([second] + starts).astype(jnp.int32)
    results = call(
        functools.partial(node_body, len(pieces), len(starts)),
        1,
        at,
        pieces,
        both(rank, 2 * rank)
        + both(2 * rank, 2 * rank, space=pltpu.HBM)
        + both(2 * rank, rank, space=pltpu.HBM),
        [pltpu.VMEM((2 * rank, 4 * rank), jnp.float32)],
        6 * rank * 4 * rank * rank,
    )
    return results[:2], results[2:4], results[4:]


def pair_body(base, high, low, own, *rest):
    pieces, results = rest[:-2], rest[-2:]
    held, width = pieces[0].shape[1], min(pieces[0].shape[1], results[0].shape[1])
    at = 0
    for result in results[::-1]:
        for start in range(0, result.shape[1], width):
            piece = pieces[at // held][:, at % held : at % held + width]
            result[:, start : start + width] = pair_product(
                high[...], low[...], own[:, at : at + width], piece
            )
            at += width


def reduce_pair(base, down, own, pieces):
    rank, size = own.shape
    return call(
        pair_body,
        1,
        base,
        [*down, own, *pieces],
        [f32(rank, size // 2)] * 2,
        [],
        12 * rank * rank * size,
    )


def couple_body(base, high, low, own, *rest):
    pieces, out = rest[:-1], rest[-1]
    width = pieces[0].shape[1]
    for i, piece in enumerate(pieces):
        columns = slice(i * width, (i + 1) * width)
        out[:, columns] = pair_product(high[...], low[...], own[:, columns], piece[...])


def couple(base, inverse, own, pieces):
    rank, size = own.shape
    return call(
        couple_body, 1, base, [*inverse, own, *pieces], [pltpu.HBM((2 * rank, size), jnp.float32)], [], 24 * rank * rank * size
    )[0]


def quarter_body(base, high, low, own, other, *quarters):
    reduced = pair_product(high[...], low[...], own[...], other[...])
    rows, width = quarters[0].shape
    for i, quarter in enumerate(quarters):
        row, column = divmod(i, 2)
        quarter[...] = reduced[row * rows : (row + 1) * rows, column * width : (column + 1) * width]


def reduce_quarters(base, down, own, other):
    rank, size = own.shape
    return call(
        quarter_body,
        1,
        base,
        [*down, own, other],
        [f32(rank // 2, size // 2)] * len(RINGS),
        [],
        12 * rank * rank * size,
    )


def back_body(base, high, low, coupled, *rest):
    coefficients, out = rest[:-1], rest[-1]
    at = 0
    for coefficient in coefficients:
        columns = slice(at, at + coefficient.shape[1])
        out[:, columns] = coupled[:, columns] - product(high[...], low[...], coefficient[...])
        at += coefficient.shape[1]


def back_substitute(base, back, coupled, coefficients, child):
    rank = back[0].shape[1]
    size = coupled.shape[1]
    rows = lambda p, base: (child, 0)
    return call(
        back_body,
        1,
        base,
        [(back[0], (rank, rank), rows), (back[1], (rank, rank), rows), (coupled, (rank, size), rows), *coefficients],
        [f32(rank, size)],
        [],
        6 * rank * rank * size,
    )[0]


def split_body(node, value, high, low):
    high[...], low[...] = halves(value[...])


def top_body(places, node, high, low, *rest):
    pieces, (out, c_high, c_low) = rest[:-3], rest[-3:]
    rows, width = pieces[0].shape
    for piece, (row, column, nodes) in zip(pieces, places):
        for at, mask in enumerate(nodes):
            start = pl.multiple_of((node[0] ^ mask) * 2 * rows + row * rows, rows)
            block = halves(piece[at * rows : (at + 1) * rows, :])
            columns = slice(column * width, (column + 1) * width)
            c_high[pl.ds(start, rows), columns], c_low[pl.ds(start, rows), columns] = block
    out[...] = part(high[...], c_high[...]) + (
        part(high[...], c_low[...]) + part(low[...], c_high[...])
    )


def solve_top(node, inverse, pieces, places):
    rank, order = inverse[0].shape
    width = 2 * pieces[0].shape[1]
    return call(
        functools.partial(top_body, places),
        1,
        node,
        [*inverse, *pieces],
        [f32(rank, width)],
        [pltpu.VMEM((order, width), jnp.bfloat16)] * 2,
        6 * rank * order * width,
    )[0]


def shards(
    shots, leaf_inverse, leaf_basis, leaf_back, level_one, level_two, level_three, top_inverse
):
    rank = leaf_basis.shape[0]
    place = lax.axis_index("leaf")
    core, near, far = place & 1, place >> 1 & 1, place >> 2 & 1
    base = jnp.reshape(core << 2 | (near ^ far) << 1 | far, (1,)).astype(jnp.int32)
    node = jnp.reshape(place // TREE, (1,)).astype(jnp.int32)

    half = jnp.stack([core, base[0] & 3]).astype(jnp.int32)
    other_half = jnp.stack([1 - core, base[0] & 3]).astype(jnp.int32)

    groups = [list(range(i, i + TREE)) for i in range(0, lax.axis_size("leaf"), TREE)]
    gather = functools.partial(
        lax.all_gather, axis_name="leaf", axis_index_groups=groups, axis=0, tiled=True
    )
    one_other = swap(level_one, CORE)
    two_near = swap(level_two, X_NEAR)
    three_near, three_far = swap(level_three, X_NEAR), swap(level_three, X_FAR)

    *sent, own = reduce_leaf(base, leaf_basis, leaf_inverse, shots)
    other = [swap(piece, CORE) for piece in sent]
    down_1, inverse_1, back_1 = node_blocks(
        [level_one, one_other], [0 * core, 0 * core + rank], core, rank
    )
    own, two_near, three_near, three_far = lax.optimization_barrier(
        (own, two_near, three_near, three_far)
    )
    sent, own_1 = reduce_pair(base, down_1, hbm(own), other)
    other_1 = swap(sent, X_NEAR)
    solved = [solve_leaf(half, leaf_inverse, after(shots, sent), pltpu.HBM)]
    three_near = after(three_near, sent)
    three_both = swap(three_near, X_FAR)
    other_1, three_both, solved[0] = lax.optimization_barrier((other_1, three_both, solved[0]))

    rows_2, rows_3 = level_two.shape[0], level_three.shape[0]
    two = [level_two, swap(level_two, CORE), two_near, swap(two_near, CORE)]
    starts = [core * rows_2, (1 - core) * rows_2]
    down_2, inverse_2, back_2 = node_blocks(
        two, starts + [rank + start for start in starts], near, rank
    )
    sent, own_2 = reduce_pair(base, down_2, own_1, [other_1])
    other_2 = swap(sent, X_FAR)
    top = gather(after(top_inverse, sent))
    own, other, own_1, other_1 = after((own, other, own_1, other_1), sent)
    coupled_1 = couple(base, inverse_1, hbm(own), other)
    coupled_2 = couple(base, inverse_2, own_1, [other_1])
    three = [level_three, three_near, three_far, three_both]
    three += [swap(value, CORE) for value in three]
    starts = []
    for flip in (0, X_FAR, CORE, X_FAR | CORE):
        for mask in (0, X_NEAR):
            seat = place ^ mask ^ flip
            starts.append(((seat ^ far << 2) >> 2 & 1) * rank + (seat & 3) * rows_3)
    down_3, inverse_3, back_3 = node_blocks(three, starts, far, rank)
    quarters = reduce_quarters(base, down_3, own_2, other_2)

    held, order = [[quarter] for quarter in quarters], [[0] for _ in RINGS]
    for step in range(len(RINGS)):
        sent = [jnp.concatenate(parts, 0) if step else parts[0] for parts in held]
        if step == len(RINGS) - 1:
            sent[-1], top = lax.optimization_barrier((sent[-1], top))
        for quarter in range(len(RINGS)):
            way = RINGS[(quarter + step) % len(RINGS)]
            held[quarter].append(swap(sent[quarter], way))
            order[quarter] += [mask ^ way for mask in order[quarter]]
        if step == 0:
            coupled_3 = couple(base, inverse_3, own_2, [other_2])
    unit = rank // ROW_STEPS
    block = ((unit, top.shape[1]), lambda p, node: (p, 0))
    top_rows = call(
        split_body,
        ROW_STEPS,
        node,
        [(hbm(top), *block)],
        [(value, *block) for value in both(*top.shape)],
        [],
        rank * top.shape[1],
    )
    pieces, places = [], []
    for quarter, parts in enumerate(held):
        row, column = divmod(quarter, 2)
        at = 0
        for value in parts:
            count = value.shape[0] // (rank // 2)
            pieces.append(value)
            places.append((row, column, [mask // TREE for mask in order[quarter][at : at + count]]))
            at += count
    coefficients = [solve_top(node, top_rows, pieces, places)]
    levels = ((coupled_3, back_3, X_FAR), (coupled_2, back_2, X_NEAR), (coupled_1, back_1, CORE))
    for coupled, back, mask in levels:
        sent = back_substitute(base, back, coupled, coefficients, 1)
        other = swap(sent, mask)
        own = back_substitute(base, back, coupled, coefficients, 0)
        if mask == X_NEAR:
            solved.append(solve_leaf(other_half, leaf_inverse, after(shots, sent), jax.ShapeDtypeStruct))
            other, solved[1] = lax.optimization_barrier((other, solved[1]))
        coefficients = [own, other]
    total = finish(half, leaf_back, own, solved[0], None)
    return finish(other_half, leaf_back, other, solved[1], total)


def solution(mesh):
    return jax.shard_map(
        shards,
        mesh=mesh,
        in_specs=(P("leaf", None),) * 8,
        out_specs=P("leaf", None),
        check_vma=False,
    )
```
